32 devices in a mesh: rows: 16 (over z, y, x), cols: 2 (over core).
Axes of the slice: x: 2, y: 2, z: 4, core: 2. Of those that a mesh axis runs over, the one named last changes fastest.
Arguments:
- tokens_in: bfloat16 [6304, 768], P(('rows', 'cols')), may hold values from -6 to 6
- ln1_gain: float32 [768], replicated, may hold values from 0.5 to 1.5
- ln1_shift: float32 [768], replicated, may hold values from -4 to 4
- qkv_weight: bfloat16 [768, 2304], P(None, 'cols'), may hold values from -0.21875 to 0.21875
- out_weight: bfloat16 [768, 768], P('cols'), may hold values from -1.75 to 1.75
- ln2_gain: float32 [768], replicated, may hold values from 0.5 to 1.5
- ln2_shift: float32 [768], replicated, may hold values from -4 to 4
- router_weight: bfloat16 [768, 32], replicated, may hold values from -0.4375 to 0.4375
- expert_in: bfloat16 [768, 98304], P(None, ('rows', 'cols')), may hold values from -0.21875 to 0.21875
- expert_out: bfloat16 [98304, 768], P(('rows', 'cols')), may hold values from -0.4375 to 0.4375
- routes: int32 [6304, 2], P(('rows', 'cols')), may hold values from 0 to 31, all different within a row; in each aligned block of 197 rows (0 to 196, 197 to 393, ...) at most 16 rows name the same one
- cotangent: bfloat16 [6304, 768], P(('rows', 'cols')), may hold values from -6 to 6
Outputs:
- output: bfloat16 [6304, 768], P(('rows', 'cols'))
- tokens_grad: bfloat16 [6304, 768], P(('rows', 'cols'))
- ln1_gain_grad: float32 [768], replicated
- ln1_shift_grad: float32 [768], replicated
- qkv_grad: float32 [768, 2304], P(None, 'cols')
- out_grad: float32 [768, 768], P('cols')
- ln2_gain_grad: float32 [768], replicated
- ln2_shift_grad: float32 [768], replicated
- router_grad: float32 [768, 32], replicated
- expert_in_grad: float32 [768, 98304], P(None, ('rows', 'cols'))
- expert_out_grad: float32 [98304, 768], P(('rows', 'cols'))
The draws below stay inside these ranges and needn't reach their ends.
Inputs may be any that keep to these rules, and one draw needn't show every extreme that they name: `routes`: the two experts of a token differ. Among the tokens of one device (aligned blocks of 197 rows) each expert is named by at most 16 assignments, a bound that some block reaches.
All inputs are finite; a program needn't handle non-finite values.
Results may differ from the reference program's by a relative error of at most 0.022.
Values may be sent and summed in bfloat16 or wider, within the bound.
A program may use at most 192 MiB of HBM per device.

```python
import math
import jax
import jax.numpy as jnp
import numpy as np
from jax import lax

D = 768
HEADS = 12
DH = 64
FF = 3072
EXPERTS = 32
SEQ = 197
TOK_DEV = 197
TOKENS = 6304
CAP = 16
N_ROWS = 16
N_COLS = 2


def levels(stream_key, dims, pieces, least, top_value):
    gain, own = 1.0, jax.random.fold_in(stream_key, 6)
    for dim, blocks in pieces:
        steps = jnp.exp(jax.random.uniform(jax.random.fold_in(own, dim), (blocks,), jnp.float32, least / len(pieces), top_value / len(pieces)))
        gain = gain * jnp.repeat(steps, dims[dim] // blocks).reshape([-1 if axis == dim else 1 for axis in range(len(dims))])
    return gain


def assign_block(key, own, number, rows, amount, top, limit, slope):
    order = jax.random.permutation(key, amount)
    heavy_load, usual = portions_of(amount, rows * top, limit, slope, True), portions_of(amount, rows * top, limit, slope, False)
    places = jnp.arange(amount)

    def named(lengths, rotation):
        used = int((lengths > 0).sum())
        fixed = max(1, used // 4)
        shifted = fixed + (places - fixed + rotation * (used - fixed)) % max(1, amount - fixed)
        return jnp.zeros((amount,), jnp.int32).at[order[jnp.where(places < fixed, places, shifted)]].set(jnp.asarray(lengths, jnp.int32))

    lengths = jnp.where(number % 4 == 0, named(heavy_load, number // 4), named(usual, number - number // 4 - 1))
    mixed = jax.random.permutation(jax.random.fold_in(own, 3), amount)
    donor, sink = mixed[0:amount // 2 * 2:2], mixed[1:amount // 2 * 2:2]
    slack = jnp.minimum(lengths[donor] - 1, limit - lengths[sink]) // 2
    slack = jnp.where((donor == order[0]) | (sink == order[0]) | (lengths[sink] == 0), 0, jnp.maximum(slack, 0))
    shifted = jax.random.randint(jax.random.fold_in(own, 4), (amount // 2,), 0, 1 << 20) % (slack + 1)
    lengths = lengths.at[donor].add(-shifted).at[sink].add(shifted)
    members = jnp.searchsorted(jnp.cumsum(lengths), jnp.arange(rows * top), side="right").astype(jnp.int32)
    grid = members.reshape(top, rows).T
    grid = grid[jax.random.permutation(jax.random.fold_in(own, 1), rows)]
    rotation = jax.random.randint(jax.random.fold_in(own, 2), (rows, 1), 0, top)
    return jnp.take_along_axis(grid, (jnp.arange(top)[None, :] + rotation) % top, axis=1)


def portions_of(number_of, total, bound, slope, full):
    loads = [(1 << 20) // math.isqrt(rank ** slope) + 1 for rank in range(1, number_of + 1)]
    largest = bound if full else min(bound, max(-(-total // number_of), total * loads[0] // sum(loads)))
    least = 1 if total - largest >= number_of - 1 else 0
    given, surplus = [largest] + [least] * (number_of - 1), total - largest - least * (number_of - 1)
    while surplus > 0:
        free = [i for i in range(1, number_of) if given[i] < largest] or [i for i in range(1, number_of) if given[i] < bound]
        mass, left = sum([loads[i] for i in free]), surplus
        for i in free:
            more = min(bound - given[i], max(1, left * loads[i] // mass), surplus)
            given[i] = given[i] + more
            surplus = surplus - more
    return np.array(given)


def noise(stream_key, dims, deviation, most, split=(), kind=jnp.bfloat16):
    entries = jax.random.normal(stream_key, dims, jnp.float32) * deviation
    if len(split) > 0:
        entries = levels(stream_key, dims, split, -0.22, 0.18) * entries
    return jnp.clip(entries, min=-most, max=most).astype(kind)


def setup_inputs(seed: int = 0) -> dict:
    key_of = jax.random.split(jax.random.key(seed), 13)
    tokens_in = noise(key_of[0], (TOKENS, D), 1.0, 6.0, ((0, 32),))
    ln1_gain = jnp.clip(1.0 + 0.1 * jax.random.normal(key_of[1], (D,), jnp.float32), 0.5, 1.5)
    ln1_shift = noise(key_of[2], (D,), 0.3, 4.0, (), jnp.float32)
    qkv_weight = noise(key_of[3], (D, 3 * D), D ** -0.5, 0.21875, ((1, 2),))
    out_weight = noise(key_of[4], (D, D), (D // 64) ** -0.5, 1.75, ((0, 2),))
    ln2_gain = jnp.clip(1.0 + 0.1 * jax.random.normal(key_of[5], (D,), jnp.float32), 0.5, 1.5)
    ln2_shift = noise(key_of[6], (D,), 0.3, 4.0, (), jnp.float32)
    router_weight = noise(key_of[7], (D, EXPERTS), (D // 4) ** -0.5, 0.4375)
    expert_in = noise(key_of[8], (D, EXPERTS * FF), D ** -0.5, 0.21875, ((1, 32),))
    expert_out = noise(key_of[9], (EXPERTS * FF, D), (FF // 16) ** -0.5, 0.4375, ((0, 32),))
    routes_keys = jax.random.split(jax.random.fold_in(key_of[10], 1), TOKENS // TOK_DEV)
    routes_turns = jax.random.permutation(jax.random.fold_in(key_of[10], 3), TOKENS // TOK_DEV)
    routes = jax.vmap(lambda own, number: assign_block(jax.random.fold_in(key_of[10], 2), own, number, TOK_DEV, EXPERTS, 2, CAP, 1))(routes_keys, routes_turns).reshape((TOKENS, 2))
    cotangent = noise(key_of[11], (TOKENS, D), 1.0, 6.0, ((0, 32),))
    return dict(tokens_in=tokens_in, ln1_gain=ln1_gain, ln1_shift=ln1_shift, qkv_weight=qkv_weight, out_weight=out_weight, ln2_gain=ln2_gain, ln2_shift=ln2_shift, router_weight=router_weight, expert_in=expert_in, expert_out=expert_out, routes=routes, cotangent=cotangent)


@jax.custom_vjp
def low(v):
    return lax.optimization_barrier(v.astype(jnp.bfloat16)).astype(jnp.float32)

@jax.custom_vjp
def low_back(v):
    return v

def low_keep(v):
    return (low(v), None)

def low_pass(kept, grad):
    return (grad,)

def back_keep(v):
    return (v, None)

def back_low(kept, grad):
    return (low(grad),)
low.defvjp(low_keep, low_pass)
low_back.defvjp(back_keep, back_low)
EPSILON = 1e-06
HIGHEST = lax.Precision.HIGHEST

def layer_norm(values, norm_gain, norm_shift):
    average = lax.optimization_barrier(jnp.mean(values, axis=-1, keepdims=True))
    centred = values - average
    variance = lax.optimization_barrier(jnp.mean(centred * centred, axis=-1, keepdims=True))
    return centred * lax.rsqrt(variance + EPSILON) * norm_gain + norm_shift

def attend(image_block):
    head_split = image_block.reshape(-1, SEQ, HEADS, 3, DH)
    queries = head_split[:, :, :, 0]
    keys_all = head_split[:, :, :, 1]
    values_all = head_split[:, :, :, 2]
    scores = low_back(jnp.einsum('nqhd,nkhd->nhqk', queries, keys_all, precision=HIGHEST) * DH ** (-0.5))
    attn_probs = jax.nn.softmax(scores, axis=-1)
    context = jnp.einsum('nhqk,nkhd->nqhd', low(attn_probs), values_all, precision=HIGHEST)
    return context.reshape(image_block.shape[0], D)

def apply_expert(operands):
    slot_rows, first_pieces, second_pieces = operands
    total = jnp.zeros((slot_rows.shape[0], D), jnp.float32)
    for piece in range(first_pieces.shape[0]):
        piece_rows = low_back(slot_rows)
        pre_act = low_back(jnp.dot(piece_rows, first_pieces[piece], precision=HIGHEST))
        act_low = low(jax.nn.gelu(pre_act, approximate=False))
        total = total + low_back(low(jnp.dot(act_low, second_pieces[piece], precision=HIGHEST)))
    return total

def slot_places(routes):
    blocks = routes.reshape(N_ROWS * N_COLS, 2 * TOK_DEV)
    expert_ids = jnp.arange(EXPERTS, dtype=jnp.int32)

    def ranks_of(route_block):
        one_hot = (route_block[:, None] == expert_ids[None, :]).astype(jnp.int32)
        return lax.optimization_barrier(jnp.sum(jnp.cumsum(one_hot, axis=0) * one_hot, axis=1)) - 1
    slot_ranks = lax.map(ranks_of, blocks)
    devices = jnp.arange(N_ROWS * N_COLS, dtype=jnp.int32)[:, None]
    return (devices * CAP + slot_ranks).reshape(-1).astype(jnp.int32)

def reference(tokens_in, ln1_gain, ln1_shift, qkv_weight, out_weight, ln2_gain, ln2_shift, router_weight, expert_in, expert_out, routes, cotangent):
    places = slot_places(routes)
    flat_ids = routes.reshape(-1).astype(jnp.int32)
    copies = max(1, N_ROWS // EXPERTS)
    part_units = FF // copies

    def forward(tokens, gain_one, shift_one, qkv_mat, out_mat, gain_two, shift_two, router_mat, first_mats, second_mats):
        normed = low(layer_norm(tokens, gain_one, shift_one))
        qkv = low_back(low(jnp.dot(normed, qkv_mat, precision=HIGHEST)))
        blocks = qkv.reshape(N_ROWS, N_COLS * TOK_DEV, 3 * D)
        context = lax.map(jax.checkpoint(attend), blocks).reshape(TOKENS, D)
        context = low_back(low(context))
        attn_out = low_back(jnp.dot(context, out_mat, precision=HIGHEST))
        hidden = tokens + attn_out
        mixed = low(layer_norm(hidden, gain_two, shift_two))
        logits = low_back(jnp.dot(mixed, router_mat, precision=HIGHEST))
        router_probs = jax.nn.softmax(logits, axis=-1)
        gate_values = jnp.take_along_axis(router_probs, routes, axis=1)
        slot_rows = jnp.repeat(mixed, 2, axis=0)
        buffers = jnp.zeros((EXPERTS, N_ROWS * N_COLS * CAP, D), jnp.float32).at[flat_ids, places].set(slot_rows)
        first_pieces = first_mats.reshape(D, EXPERTS, copies, part_units).transpose(1, 2, 0, 3)
        second_pieces = second_mats.reshape(EXPERTS, copies, part_units, D)
        results = lax.map(jax.checkpoint(apply_expert), (buffers, first_pieces, second_pieces))
        picked = results[flat_ids, places].reshape(TOKENS, 2, D)
        return hidden + lax.optimization_barrier(jnp.sum(gate_values[:, :, None] * picked, axis=1))
    output, pullback = jax.vjp(forward, tokens_in.astype(jnp.float32), ln1_gain.astype(jnp.float32), ln1_shift.astype(jnp.float32), qkv_weight.astype(jnp.float32), out_weight.astype(jnp.float32), ln2_gain.astype(jnp.float32), ln2_shift.astype(jnp.float32), router_weight.astype(jnp.float32), expert_in.astype(jnp.float32), expert_out.astype(jnp.float32))
    grads = pullback(cotangent.astype(jnp.float32))
    return (output.astype(jnp.bfloat16), grads[0].astype(jnp.bfloat16), grads[1], grads[2], grads[3], grads[4], grads[5], grads[6], grads[7], grads[8], grads[9])
```

```python
import jax
import jax.numpy as jnp
from jax import lax
from jax.experimental import pallas as pl
from jax.experimental.pallas import tpu as pltpu
from jax.sharding import PartitionSpec as P

DH = 64
FF = 3072
SEQ = 197


EPSILON = 1e-06


def layer_norm(values, norm_gain, norm_shift):
    average = jnp.mean(values, axis=-1, keepdims=True)
    centred = values - average
    variance = jnp.mean(centred * centred, axis=-1, keepdims=True)
    return centred * lax.rsqrt(variance + EPSILON) * norm_gain + norm_shift


def gelu_slope(pre_act):
    normal_cdf = 0.5 * (1.0 + jax.scipy.special.erf(pre_act * 0.7071067811865476))
    density = jnp.exp(-0.5 * pre_act * pre_act) * 0.3989422804014327
    return normal_cdf + pre_act * density


def dot_rows(first_side, second_side):
    return lax.dot_general(
        first_side, second_side, (((0,), (0,)), ((), ())), preferred_element_type=jnp.float32
    )


def dot_last(first_side, second_side):
    return lax.dot_general(
        first_side, second_side, (((1,), (1,)), ((), ())), preferred_element_type=jnp.float32
    )


def bit_orders(bits):
    cycle = list(range(bits - 1))
    return [cycle[turn:] + cycle[:turn] + [bits - 1] for turn in range(3)]


def sum_kernel(
    qkv_ref,
    out_ref,
    small_ref,
    qkv_sum,
    out_sum,
    small_sum,
    qkv_acc,
    out_acc,
    qkv_got,
    out_got,
    small_acc,
    small_got,
    send_sems,
    recv_sems,
    small_send,
    small_recv,
):
    shards = qkv_ref.shape[0]
    bits = shards.bit_length() - 1
    row_place = lax.axis_index("rows")
    col_place = lax.axis_index("cols")

    def row_partner(bit):
        here = (row_place // 2**bit) % 2
        return here, (row_place + (1 - 2 * here) * 2**bit, col_place)

    other_core = (row_place, 1 - col_place)
    barrier = pltpu.get_barrier_semaphore()
    for bit in range(bits):
        pl.semaphore_signal(
            barrier, inc=1, device_id=row_partner(bit)[1], device_id_type=pl.DeviceIdType.MESH
        )
    pl.semaphore_signal(
        barrier, inc=1, device_id=other_core, device_id_type=pl.DeviceIdType.MESH
    )
    pl.semaphore_wait(barrier, bits + 1)

    width = qkv_ref.shape[2]
    third = (width * qkv_ref.shape[1] + out_ref.shape[2] * out_ref.shape[1]) // (
        3 * qkv_ref.shape[1]
    )
    third = min(third // 128 * 128, width // 2)
    orders = bit_orders(bits)
    streams = [
        (qkv_ref, qkv_acc, qkv_got, qkv_sum, pl.ds(0, third), orders[0]),
        (qkv_ref, qkv_acc, qkv_got, qkv_sum, pl.ds(third, third), orders[1]),
        (out_ref, out_acc, out_got, out_sum, pl.ds(0, out_ref.shape[2]), orders[2]),
    ]
    if width > 2 * third:
        last = pl.ds(2 * third, width - 2 * third)
        streams.append((qkv_ref, qkv_acc, qkv_got, qkv_sum, last, orders[2]))
    bases = [0 for unused in streams]

    def send(source, target, place, step, device):
        copy = pltpu.make_async_remote_copy(
            src_ref=source,
            dst_ref=target,
            send_sem=send_sems.at[place, step],
            recv_sem=recv_sems.at[place, step],
            device_id=device,
            device_id_type=pl.DeviceIdType.MESH,
        )
        copy.start()
        return copy

    small_acc[0] = small_ref[...]

    def small_send_start(step):
        device = row_partner(step)[1] if step < bits else other_core
        copy = pltpu.make_async_remote_copy(
            src_ref=small_acc.at[step],
            dst_ref=small_got.at[step],
            send_sem=small_send.at[step],
            recv_sem=small_recv.at[step],
            device_id=device,
            device_id_type=pl.DeviceIdType.MESH,
        )
        copy.start()
        return copy

    def small_finish(step, copy):
        copy.wait()
        small_acc[step + 1] = small_acc[step] + small_got[step]

    got_base = 0
    half = shards
    for step in range(bits):
        half = half // 2
        copies = []
        for place, (ref, acc, got, total, cols, order) in enumerate(streams):
            here, device = row_partner(order[step])
            source = ref if step == 0 else acc
            give = bases[place] + (1 - here) * half
            bases[place] = bases[place] + here * half
            copies.append(
                send(
                    source.at[pl.ds(give, half), :, cols],
                    got.at[pl.ds(got_base, half), :, cols],
                    place,
                    step,
                    device,
                )
            )
        small_copy = small_send_start(step)
        for place, (ref, acc, got, total, cols, order) in enumerate(streams):
            copies[place].wait()
            source = ref if step == 0 else acc
            keep = bases[place]

            def add(index, unused, source=source, acc=acc, got=got, cols=cols, keep=keep, start=got_base):
                acc[keep + index, :, cols] = (
                    source[keep + index, :, cols].astype(jnp.float32)
                    + got[start + index, :, cols].astype(jnp.float32)
                ).astype(jnp.bfloat16)
                return unused

            lax.fori_loop(0, half, add, 0)
        small_finish(step, small_copy)
        got_base += half
    small_copy = small_send_start(bits)
    for place, (ref, acc, got, total, cols, order) in enumerate(streams):
        total[bases[place], :, cols] = acc[bases[place], :, cols]
    held = 1
    for step in reversed(range(bits)):
        copies = []
        for place, (ref, acc, got, total, cols, order) in enumerate(streams):
            here, device = row_partner(order[step])
            block = total.at[pl.ds(bases[place], held), :, cols]
            copies.append(send(block, block, place, 2 * bits - 1 - step, device))
            bases[place] = bases[place] - here * held
        for copy in copies:
            copy.wait()
        held = 2 * held
    small_finish(bits, small_copy)
    small_sum[...] = small_acc[bits + 1]


def sum_over_devices(qkv_part, out_part, small_part):
    shards = lax.axis_size("rows")
    bits = shards.bit_length() - 1
    qkv_shape = (shards, qkv_part.shape[0] // shards, qkv_part.shape[1])
    out_shape = (shards, out_part.shape[0] // shards, out_part.shape[1])
    small_shape = small_part.shape
    in_vmem = pl.BlockSpec(memory_space=pltpu.VMEM)
    qkv_sum, out_sum, small_sum = pl.pallas_call(
        sum_kernel,
        out_shape=(
            jax.ShapeDtypeStruct(qkv_shape, jnp.bfloat16),
            jax.ShapeDtypeStruct(out_shape, jnp.bfloat16),
            jax.ShapeDtypeStruct(small_shape, jnp.float32),
        ),
        in_specs=[in_vmem] * 3,
        out_specs=(in_vmem,) * 3,
        scratch_shapes=[
            pltpu.VMEM(qkv_shape, jnp.bfloat16),
            pltpu.VMEM(out_shape, jnp.bfloat16),
            pltpu.VMEM(qkv_shape, jnp.bfloat16),
            pltpu.VMEM(out_shape, jnp.bfloat16),
            pltpu.VMEM((bits + 2, *small_shape), jnp.float32),
            pltpu.VMEM((bits + 1, *small_shape), jnp.float32),
            pltpu.SemaphoreType.DMA((4, 2 * bits)),
            pltpu.SemaphoreType.DMA((4, 2 * bits)),
            pltpu.SemaphoreType.DMA((bits + 1,)),
            pltpu.SemaphoreType.DMA((bits + 1,)),
        ],
        compiler_params=pltpu.CompilerParams(collective_id=0, has_side_effects=True),
        name="sum_gradients",
    )(qkv_part.reshape(qkv_shape), out_part.reshape(out_shape), small_part)
    return (
        qkv_sum.astype(jnp.float32).reshape(qkv_part.shape),
        out_sum.astype(jnp.float32).reshape(out_part.shape),
        small_sum,
    )


def attention_scores(queries, keys_all, score_scale):
    scores = jnp.einsum("nqhd,nkhd->nhqk", queries, keys_all, preferred_element_type=jnp.float32)
    return scores * score_scale


def share_over_cores(parts, col_place):
    theirs = lax.dynamic_index_in_dim(parts, 1 - col_place, 0, keepdims=False)
    ours = lax.dynamic_index_in_dim(parts, col_place, 0, keepdims=False)
    return ours, lax.ppermute(theirs, "cols", [(0, 1), (1, 0)])


def body(
    tokens_in,
    ln1_gain,
    ln1_shift,
    qkv_weight,
    out_weight,
    ln2_gain,
    ln2_shift,
    router_weight,
    expert_in,
    expert_out,
    routes,
    cotangent,
):
    local_rows = tokens_in.shape[0]
    model_width = tokens_in.shape[1]
    experts = router_weight.shape[1]
    capacity = max(2, 8 * local_rows // (3 * experts))
    heads_local = qkv_weight.shape[1] // (3 * DH)
    score_scale = DH ** (-0.5)
    row_place = lax.axis_index("rows")
    col_place = lax.axis_index("cols")
    device_count = lax.axis_size("rows") * lax.axis_size("cols")
    copies = device_count // experts
    slot_ids = jnp.arange(device_count * capacity, dtype=jnp.int32)
    slot_expert = slot_ids // (capacity * copies)
    names_slot = [routes[:, k][:, None] == slot_expert[None, :] for k in range(2)]
    token_ids = jnp.arange(local_rows, dtype=jnp.int32)
    earlier = (token_ids[None, :] < token_ids[:, None]).astype(jnp.bfloat16)
    slot_ranks = jnp.dot(
        earlier,
        (names_slot[0] | names_slot[1]).astype(jnp.bfloat16),
        preferred_element_type=jnp.float32,
    )
    in_slot = slot_ranks == (slot_ids % capacity).astype(jnp.float32)[None, :]
    place_one = (names_slot[0] & in_slot).astype(jnp.bfloat16)
    place_two = (names_slot[1] & in_slot).astype(jnp.bfloat16)
    place_any = place_one + place_two

    def to_experts(token_rows):
        filled = dot_rows(place_any, token_rows).astype(jnp.bfloat16)
        return swap_slots(filled)

    def swap_slots(slot_rows):
        swapped = lax.all_to_all(
            slot_rows.reshape(device_count, capacity, model_width),
            ("rows", "cols"),
            split_axis=0,
            concat_axis=0,
            tiled=True,
        )
        return swapped.reshape(device_count * capacity, model_width)

    cotangent_arrived = to_experts(cotangent)
    tokens_f = tokens_in.astype(jnp.float32)
    normed_low = layer_norm(tokens_f, ln1_gain, ln1_shift).astype(jnp.bfloat16)
    gathered = lax.all_gather(normed_low, "cols", axis=0, tiled=True)
    pair_rows = gathered.shape[0]
    images = pair_rows // SEQ
    qkv_low = jnp.dot(gathered, qkv_weight, preferred_element_type=jnp.float32).astype(jnp.bfloat16)
    head_split = qkv_low.reshape(images, SEQ, heads_local, 3, DH)
    queries = head_split[:, :, :, 0]
    keys_all = head_split[:, :, :, 1]
    values_all = head_split[:, :, :, 2]
    scores = attention_scores(queries, keys_all, score_scale)
    score_peak = jnp.max(scores, axis=-1, keepdims=True)
    log_total = score_peak + jnp.log(jnp.sum(jnp.exp(scores - score_peak), axis=-1, keepdims=True))
    weights_low = jnp.exp(scores - log_total).astype(jnp.bfloat16)
    context = jnp.einsum(
        "nhqk,nkhd->nqhd", weights_low, values_all, preferred_element_type=jnp.float32
    )
    context_low = context.astype(jnp.bfloat16).reshape(pair_rows, heads_local * DH)
    attn_parts = jnp.dot(context_low, out_weight, preferred_element_type=jnp.float32)
    attn_ours, attn_theirs = share_over_cores(
        attn_parts.reshape(images, SEQ, model_width), col_place
    )
    attn_out = attn_ours + attn_theirs
    hidden_one = tokens_f + attn_out
    mixed_low = layer_norm(hidden_one, ln2_gain, ln2_shift).astype(jnp.bfloat16)
    logits = jnp.dot(mixed_low, router_weight, preferred_element_type=jnp.float32)
    router_probs = jax.nn.softmax(logits, axis=-1)
    expert_ids = jnp.arange(experts, dtype=jnp.int32)
    chosen = (routes[:, :, None] == expert_ids[None, None, :]).astype(jnp.float32)
    gate_values = jnp.sum(router_probs[:, None, :] * chosen, axis=-1)
    grad_out = cotangent.astype(jnp.float32)
    arrived = to_experts(mixed_low)
    own_expert = (row_place * lax.axis_size("cols") + col_place) // copies
    arrived_probs = jax.nn.softmax(
        jnp.dot(arrived, router_weight, preferred_element_type=jnp.float32), axis=-1
    )
    arrived_gate = jnp.sum(
        jnp.where(expert_ids[None, :] == own_expert, arrived_probs, 0.0), axis=-1, keepdims=True
    )
    grad_result = (arrived_gate * cotangent_arrived.astype(jnp.float32)).astype(jnp.bfloat16)
    pre_act = jnp.dot(arrived, expert_in, preferred_element_type=jnp.float32)
    act_low = jax.nn.gelu(pre_act, approximate=False).astype(jnp.bfloat16)
    result_low = jnp.dot(act_low, expert_out, preferred_element_type=jnp.float32).astype(
        jnp.bfloat16
    )
    returned = swap_slots(result_low)
    grad_act = dot_last(grad_result, expert_out)
    grad_pre_low = (grad_act * gelu_slope(pre_act)).astype(jnp.bfloat16)
    grad_arrived = dot_last(grad_pre_low, expert_in).astype(jnp.bfloat16)
    grad_sent = swap_slots(grad_arrived)
    first_grad = dot_rows(arrived, grad_pre_low)
    second_grad = dot_rows(act_low, grad_result)
    picked_one = jnp.dot(place_one, returned, preferred_element_type=jnp.float32)
    picked_two = jnp.dot(place_two, returned, preferred_element_type=jnp.float32)
    output = (
        hidden_one + gate_values[:, 0:1] * picked_one + gate_values[:, 1:2] * picked_two
    ).astype(jnp.bfloat16)
    grad_gates = jnp.stack(
        [jnp.sum(grad_out * picked_one, axis=-1), jnp.sum(grad_out * picked_two, axis=-1)], axis=1
    )
    grad_mixed_experts = jnp.dot(place_any, grad_sent, preferred_element_type=jnp.float32)
    gate_term = jnp.sum(grad_gates * gate_values, axis=-1, keepdims=True)
    grad_probs = jnp.sum(chosen * grad_gates[:, :, None], axis=1)
    grad_logits_low = (router_probs * (grad_probs - gate_term)).astype(jnp.bfloat16)
    router_grad = dot_rows(grad_logits_low, mixed_low)
    grad_mixed = dot_last(grad_logits_low, router_weight) + grad_mixed_experts
    unused_two, norm_two_back = jax.vjp(layer_norm, hidden_one, ln2_gain, ln2_shift)
    grad_hidden_part, ln2_gain_grad, ln2_shift_grad = norm_two_back(grad_mixed)
    grad_hidden = grad_out + grad_hidden_part
    grad_attn_low = grad_hidden.astype(jnp.bfloat16)
    grad_attn_all = lax.all_gather(grad_attn_low, "cols", axis=0, tiled=True)
    out_grad = dot_rows(context_low, grad_attn_all)
    grad_context = (
        dot_last(grad_attn_all, out_weight)
        .astype(jnp.bfloat16)
        .reshape(images, SEQ, heads_local, DH)
    )
    scores_again = attention_scores(queries, keys_all, score_scale)
    attn_probs = jnp.exp(scores_again - log_total)
    probs_low = attn_probs.astype(jnp.bfloat16)
    grad_values = jnp.einsum(
        "nhqk,nqhd->nkhd", probs_low, grad_context, preferred_element_type=jnp.float32
    )
    grad_weights = jnp.einsum(
        "nqhd,nkhd->nhqk", grad_context, values_all, preferred_element_type=jnp.float32
    )
    row_term = jnp.sum(grad_weights * attn_probs, axis=-1, keepdims=True)
    grad_scores = (attn_probs * (grad_weights - row_term)).astype(jnp.bfloat16)
    grad_queries = (
        jnp.einsum("nhqk,nkhd->nqhd", grad_scores, keys_all, preferred_element_type=jnp.float32)
        * score_scale
    )
    grad_keys = (
        jnp.einsum("nhqk,nqhd->nkhd", grad_scores, queries, preferred_element_type=jnp.float32)
        * score_scale
    )
    grad_qkv = (
        jnp.stack([grad_queries, grad_keys, grad_values], axis=3)
        .astype(jnp.bfloat16)
        .reshape(pair_rows, 3 * heads_local * DH)
    )
    qkv_grad = dot_rows(gathered, grad_qkv)
    normed_ours, normed_theirs = share_over_cores(
        dot_last(grad_qkv, qkv_weight).astype(jnp.bfloat16).reshape(images, SEQ, model_width),
        col_place,
    )
    grad_normed = normed_ours.astype(jnp.float32) + normed_theirs.astype(jnp.float32)
    unused_one, norm_one_back = jax.vjp(layer_norm, tokens_f, ln1_gain, ln1_shift)
    grad_tokens_part, ln1_gain_grad, ln1_shift_grad = norm_one_back(grad_normed)
    tokens_grad = (grad_hidden + grad_tokens_part).astype(jnp.bfloat16)
    small_part = jnp.concatenate(
        [
            router_grad,
            ln1_gain_grad[None],
            ln1_shift_grad[None],
            ln2_gain_grad[None],
            ln2_shift_grad[None],
            jnp.zeros((4, model_width), jnp.float32),
        ],
        axis=0,
    )
    qkv_grad, out_grad, small_sum = sum_over_devices(
        qkv_grad.astype(jnp.bfloat16), out_grad.astype(jnp.bfloat16), small_part
    )
    router_grad = small_sum[:experts].T
    ln1_gain_grad, ln1_shift_grad, ln2_gain_grad, ln2_shift_grad = (
        small_sum[experts],
        small_sum[experts + 1],
        small_sum[experts + 2],
        small_sum[experts + 3],
    )
    return (
        output,
        tokens_grad,
        ln1_gain_grad,
        ln1_shift_grad,
        qkv_grad,
        out_grad,
        ln2_gain_grad,
        ln2_shift_grad,
        router_grad,
        first_grad,
        second_grad,
    )


def solution(mesh):
    in_specs = (
        P(("rows", "cols"), None),
        P(),
        P(),
        P(None, "cols"),
        P("cols", None),
        P(),
        P(),
        P(),
        P(None, ("rows", "cols")),
        P(("rows", "cols"), None),
        P(("rows", "cols"), None),
        P(("rows", "cols"), None),
    )
    out_specs = (
        P(("rows", "cols"), None),
        P(("rows", "cols"), None),
        P(),
        P(),
        P(None, "cols"),
        P("cols", None),
        P(),
        P(),
        P(),
        P(None, ("rows", "cols")),
        P(("rows", "cols"), None),
    )
    return jax.shard_map(body, mesh=mesh, in_specs=in_specs, out_specs=out_specs, check_vma=False)
```

```python
import jax
import jax.numpy as jnp
from jax import lax
from jax.experimental import pallas as pl
from jax.experimental.pallas import tpu as pltpu
from jax.sharding import PartitionSpec as P

DH = 64
FF = 3072
SEQ = 197


EPSILON = 1e-06


def layer_norm(values, norm_gain, norm_shift):
    average = jnp.mean(values, axis=-1, keepdims=True)
    centred = values - average
    variance = jnp.mean(centred * centred, axis=-1, keepdims=True)
    return centred * lax.rsqrt(variance + EPSILON) * norm_gain + norm_shift


def gelu_slope(pre_act):
    normal_cdf = 0.5 * (1.0 + jax.scipy.special.erf(pre_act * 0.7071067811865476))
    density = jnp.exp(-0.5 * pre_act * pre_act) * 0.3989422804014327
    return normal_cdf + pre_act * density


def dot_rows(first_side, second_side):
    return lax.dot_general(
        first_side, second_side, (((0,), (0,)), ((), ())), preferred_element_type=jnp.float32
    )


def dot_last(first_side, second_side):
    return lax.dot_general(
        first_side, second_side, (((1,), (1,)), ((), ())), preferred_element_type=jnp.float32
    )


def bit_orders(bits):
    cycle = list(range(bits - 1))
    return [cycle[turn:] + cycle[:turn] + [bits - 1] for turn in range(3)]


def sum_kernel(
    qkv_ref,
    out_ref,
    small_ref,
    qkv_sum,
    out_sum,
    small_sum,
    qkv_acc,
    out_acc,
    qkv_got,
    out_got,
    small_acc,
    small_got,
    send_sems,
    recv_sems,
    small_send,
    small_recv,
):
    shards = qkv_ref.shape[0]
    bits = shards.bit_length() - 1
    row_place = lax.axis_index("rows")
    col_place = lax.axis_index("cols")

    def row_partner(bit):
        here = (row_place // 2**bit) % 2
        return here, (row_place + (1 - 2 * here) * 2**bit, col_place)

    other_core = (row_place, 1 - col_place)
    barrier = pltpu.get_barrier_semaphore()
    for bit in range(bits):
        pl.semaphore_signal(
            barrier, inc=1, device_id=row_partner(bit)[1], device_id_type=pl.DeviceIdType.MESH
        )
    pl.semaphore_signal(
        barrier, inc=1, device_id=other_core, device_id_type=pl.DeviceIdType.MESH
    )
    pl.semaphore_wait(barrier, bits + 1)

    width = qkv_ref.shape[2]
    third = (width * qkv_ref.shape[1] + out_ref.shape[2] * out_ref.shape[1]) // (
        3 * qkv_ref.shape[1]
    )
    third = min(third // 128 * 128, width // 2)
    orders = bit_orders(bits)
    streams = [
        (qkv_ref, qkv_acc, qkv_got, qkv_sum, pl.ds(0, third), orders[0]),
        (qkv_ref, qkv_acc, qkv_got, qkv_sum, pl.ds(third, third), orders[1]),
        (out_ref, out_acc, out_got, out_sum, pl.ds(0, out_ref.shape[2]), orders[2]),
    ]
    if width > 2 * third:
        last = pl.ds(2 * third, width - 2 * third)
        streams.append((qkv_ref, qkv_acc, qkv_got, qkv_sum, last, orders[2]))
    bases = [0 for unused in streams]

    def send(source, target, place, step, device):
        copy = pltpu.make_async_remote_copy(
            src_ref=source,
            dst_ref=target,
            send_sem=send_sems.at[place, step],
            recv_sem=recv_sems.at[place, step],
            device_id=device,
            device_id_type=pl.DeviceIdType.MESH,
        )
        copy.start()
        return copy

    small_acc[0] = small_ref[...]

    def small_send_start(step):
        device = row_partner(step)[1] if step < bits else other_core
        copy = pltpu.make_async_remote_copy(
            src_ref=small_acc.at[step],
            dst_ref=small_got.at[step],
            send_sem=small_send.at[step],
            recv_sem=small_recv.at[step],
            device_id=device,
            device_id_type=pl.DeviceIdType.MESH,
        )
        copy.start()
        return copy

    def small_finish(step, copy):
        copy.wait()
        small_acc[step + 1] = small_acc[step] + small_got[step]

    def give_half(place, step):
        ref, acc, got, total, cols, order = streams[place]
        here, device = row_partner(order[step])
        half = shards >> (step + 1)
        source = ref if step == 0 else acc
        give = bases[place] + (1 - here) * half
        bases[place] = bases[place] + here * half
        return send(
            source.at[pl.ds(give, half), :, cols],
            got.at[pl.ds(shards - 2 * half, half), :, cols],
            place,
            step,
            device,
        )

    def pass_block(place, step):
        ref, acc, got, total, cols, order = streams[place]
        here, device = row_partner(order[step])
        held = shards >> (step + 1)
        block = total.at[pl.ds(bases[place], held), :, cols]
        bases[place] = bases[place] - here * held
        return send(block, block, place, 2 * bits - 1 - step, device)

    copies = [give_half(place, 0) for place in range(len(streams))]
    small_copy = small_send_start(0)
    for step in range(bits):
        half = shards >> (step + 1)
        for place, (ref, acc, got, total, cols, order) in enumerate(streams):
            copies[place].wait()
            source = ref if step == 0 else acc
            target = acc if step < bits - 1 else total
            keep = bases[place]

            def add(index, unused, parts=(source, target, got, cols, keep, shards - 2 * half)):
                source, target, got, cols, keep, start = parts
                target[keep + index, :, cols] = (
                    source[keep + index, :, cols].astype(jnp.float32)
                    + got[start + index, :, cols].astype(jnp.float32)
                ).astype(jnp.bfloat16)
                return unused

            lax.fori_loop(0, half, add, 0)
            if step < bits - 1:
                copies[place] = give_half(place, step + 1)
            else:
                copies[place] = pass_block(place, step)
        small_finish(step, small_copy)
        small_copy = small_send_start(step + 1)
    for step in reversed(range(bits)):
        for place in range(len(streams)):
            copies[place].wait()
            if step > 0:
                copies[place] = pass_block(place, step - 1)
    small_finish(bits, small_copy)
    small_sum[...] = small_acc[bits + 1]


def sum_over_devices(qkv_part, out_part, small_part):
    shards = lax.axis_size("rows")
    bits = shards.bit_length() - 1
    qkv_shape = (shards, qkv_part.shape[0] // shards, qkv_part.shape[1])
    out_shape = (shards, out_part.shape[0] // shards, out_part.shape[1])
    small_shape = small_part.shape
    in_vmem = pl.BlockSpec(memory_space=pltpu.VMEM)
    qkv_sum, out_sum, small_sum = pl.pallas_call(
        sum_kernel,
        out_shape=(
            jax.ShapeDtypeStruct(qkv_shape, jnp.bfloat16),
            jax.ShapeDtypeStruct(out_shape, jnp.bfloat16),
            jax.ShapeDtypeStruct(small_shape, jnp.float32),
        ),
        in_specs=[in_vmem] * 3,
        out_specs=(in_vmem,) * 3,
        scratch_shapes=[
            pltpu.VMEM(qkv_shape, jnp.bfloat16),
            pltpu.VMEM(out_shape, jnp.bfloat16),
            pltpu.VMEM(qkv_shape, jnp.bfloat16),
            pltpu.VMEM(out_shape, jnp.bfloat16),
            pltpu.VMEM((bits + 2, *small_shape), jnp.float32),
            pltpu.VMEM((bits + 1, *small_shape), jnp.float32),
            pltpu.SemaphoreType.DMA((4, 2 * bits)),
            pltpu.SemaphoreType.DMA((4, 2 * bits)),
            pltpu.SemaphoreType.DMA((bits + 1,)),
            pltpu.SemaphoreType.DMA((bits + 1,)),
        ],
        compiler_params=pltpu.CompilerParams(collective_id=0, has_side_effects=True),
        name="sum_gradients",
    )(qkv_part.reshape(qkv_shape), out_part.reshape(out_shape), small_part)
    return (
        qkv_sum.astype(jnp.float32).reshape(qkv_part.shape),
        out_sum.astype(jnp.float32).reshape(out_part.shape),
        small_sum,
    )


def dot_plain(first_side, second_side):
    return jnp.dot(first_side, second_side, preferred_element_type=jnp.float32)


def key_weights(queries, keys_all):
    scores = dot_last(keys_all, queries) * DH ** (-0.5)
    key_ids = lax.broadcasted_iota(jnp.int32, scores.shape, 0)
    scores = jnp.where(key_ids < SEQ, scores, -1e30)
    powers = jnp.exp(scores - jnp.max(scores, axis=0, keepdims=True))
    return powers * (1.0 / jnp.sum(powers, axis=0, keepdims=True))


def forward_kernel(rows_ref, qkv_weight, out_weight, qkv_ref, context_ref, parts_ref, padded):
    images = rows_ref.shape[0]
    span = padded.shape[0]
    heads = qkv_weight.shape[1] // (3 * DH)

    def one_image(image, unused):
        padded[...] = jnp.zeros_like(padded)
        padded[0:SEQ, :] = rows_ref[image]
        qkv_ref[image] = dot_plain(padded[...], qkv_weight[...]).astype(jnp.bfloat16)
        for pair in range(heads // 2):
            block = qkv_ref[image, :, 6 * DH * pair : 6 * DH * (pair + 1)]
            found = []
            for head in range(2):
                base = 3 * DH * head
                weights = key_weights(
                    block[:, base : base + DH], block[:, base + DH : base + 2 * DH]
                ).astype(jnp.bfloat16)
                found.append(dot_rows(weights, block[:, base + 2 * DH : base + 3 * DH]))
            context_ref[image, :, 2 * DH * pair : 2 * DH * (pair + 1)] = jnp.concatenate(
                found, axis=1
            ).astype(jnp.bfloat16)
        parts_ref[image] = dot_plain(context_ref[image], out_weight[...])[0:SEQ]
        return unused

    lax.fori_loop(0, images, one_image, 0)


def attention_forward(rows, qkv_weight, out_weight):
    images, unused, model_width = rows.shape
    span = -(-SEQ // 128) * 128
    in_vmem = pl.BlockSpec(memory_space=pltpu.VMEM)
    return pl.pallas_call(
        forward_kernel,
        out_shape=(
            jax.ShapeDtypeStruct((images, span, qkv_weight.shape[1]), jnp.bfloat16),
            jax.ShapeDtypeStruct((images, span, out_weight.shape[0]), jnp.bfloat16),
            jax.ShapeDtypeStruct((images, SEQ, model_width), jnp.float32),
        ),
        in_specs=[in_vmem] * 3,
        out_specs=(in_vmem,) * 3,
        scratch_shapes=[pltpu.VMEM((span, model_width), jnp.bfloat16)],
        name="attention_forward",
    )(rows, qkv_weight, out_weight)


def backward_kernel(
    rows_ref,
    grad_ref,
    qkv_ref,
    context_ref,
    qkv_weight,
    out_weight,
    qkv_grad,
    out_grad,
    normed_grad,
    rows_padded,
    grad_padded,
    grad_context,
    grad_qkv,
):
    images, span = qkv_ref.shape[0], qkv_ref.shape[1]
    heads = qkv_weight.shape[1] // (3 * DH)
    scale = DH ** (-0.5)
    rows_padded[...] = jnp.zeros_like(rows_padded)
    grad_padded[...] = jnp.zeros_like(grad_padded)

    def one_image(image, unused):
        rows_padded[image, 0:SEQ, :] = rows_ref[image]
        grad_padded[image, 0:SEQ, :] = grad_ref[image]
        grad_context[...] = dot_last(grad_padded[image], out_weight[...]).astype(jnp.bfloat16)
        for pair in range(heads // 2):
            block = qkv_ref[image, :, 6 * DH * pair : 6 * DH * (pair + 1)]
            grads = grad_context[:, 2 * DH * pair : 2 * DH * (pair + 1)]
            found = []
            for head in range(2):
                base = 3 * DH * head
                queries = block[:, base : base + DH]
                keys_all = block[:, base + DH : base + 2 * DH]
                values_all = block[:, base + 2 * DH : base + 3 * DH]
                head_grad = grads[:, DH * head : DH * (head + 1)]
                weights = key_weights(queries, keys_all)
                grad_values = dot_plain(weights.astype(jnp.bfloat16), head_grad)
                grad_weights = dot_last(values_all, head_grad)
                row_term = jnp.sum(grad_weights * weights, axis=0, keepdims=True)
                grad_scores = (weights * (grad_weights - row_term)).astype(jnp.bfloat16)
                grad_queries = dot_rows(grad_scores, keys_all) * scale
                grad_keys = dot_plain(grad_scores, queries) * scale
                found += [grad_queries, grad_keys, grad_values]
            grad_qkv[image, :, 6 * DH * pair : 6 * DH * (pair + 1)] = jnp.concatenate(
                found, axis=1
            ).astype(jnp.bfloat16)
        normed_grad[image] = dot_last(grad_qkv[image], qkv_weight[...])[0:SEQ].astype(jnp.bfloat16)
        return unused

    lax.fori_loop(0, images, one_image, 0)

    def flat(ref):
        return ref[...].reshape(images * span, ref.shape[2])

    qkv_grad[...] = dot_rows(flat(rows_padded), flat(grad_qkv)).astype(jnp.bfloat16)
    out_grad[...] = dot_rows(flat(context_ref), flat(grad_padded)).astype(jnp.bfloat16)


def attention_backward(rows, grad_rows, qkv, context, qkv_weight, out_weight):
    images, unused, model_width = rows.shape
    span = qkv.shape[1]
    in_vmem = pl.BlockSpec(memory_space=pltpu.VMEM)
    return pl.pallas_call(
        backward_kernel,
        out_shape=(
            jax.ShapeDtypeStruct(qkv_weight.shape, jnp.bfloat16),
            jax.ShapeDtypeStruct(out_weight.shape, jnp.bfloat16),
            jax.ShapeDtypeStruct((images, SEQ, model_width), jnp.bfloat16),
        ),
        in_specs=[in_vmem] * 6,
        out_specs=(in_vmem,) * 3,
        scratch_shapes=[
            pltpu.VMEM((images, span, model_width), jnp.bfloat16),
            pltpu.VMEM((images, span, model_width), jnp.bfloat16),
            pltpu.VMEM((span, out_weight.shape[0]), jnp.bfloat16),
            pltpu.VMEM((images, span, qkv_weight.shape[1]), jnp.bfloat16),
        ],
        name="attention_backward",
    )(rows, grad_rows, qkv, context, qkv_weight, out_weight)


def share_over_cores(parts, col_place):
    count = parts.shape[0] // 2
    theirs = lax.dynamic_slice_in_dim(parts, (1 - col_place) * count, count, 0)
    ours = lax.dynamic_slice_in_dim(parts, col_place * count, count, 0)
    theirs = theirs.reshape(count * SEQ, -1)
    ours = ours.reshape(count * SEQ, -1)
    return ours, lax.ppermute(theirs, "cols", [(0, 1), (1, 0)])


def body(
    tokens_in,
    ln1_gain,
    ln1_shift,
    qkv_weight,
    out_weight,
    ln2_gain,
    ln2_shift,
    router_weight,
    expert_in,
    expert_out,
    routes,
    cotangent,
):
    local_rows = tokens_in.shape[0]
    model_width = tokens_in.shape[1]
    experts = router_weight.shape[1]
    capacity = max(2, 8 * local_rows // (3 * experts))
    row_place = lax.axis_index("rows")
    col_place = lax.axis_index("cols")
    device_count = lax.axis_size("rows") * lax.axis_size("cols")
    copies = device_count // experts
    slot_ids = jnp.arange(device_count * capacity, dtype=jnp.int32)
    slot_expert = slot_ids // (capacity * copies)
    names_slot = [routes[:, k][:, None] == slot_expert[None, :] for k in range(2)]
    token_ids = jnp.arange(local_rows, dtype=jnp.int32)
    earlier = (token_ids[None, :] < token_ids[:, None]).astype(jnp.bfloat16)
    slot_ranks = jnp.dot(
        earlier,
        (names_slot[0] | names_slot[1]).astype(jnp.bfloat16),
        preferred_element_type=jnp.float32,
    )
    in_slot = slot_ranks == (slot_ids % capacity).astype(jnp.float32)[None, :]
    place_one = (names_slot[0] & in_slot).astype(jnp.bfloat16)
    place_two = (names_slot[1] & in_slot).astype(jnp.bfloat16)
    place_any = place_one + place_two

    def to_experts(token_rows):
        filled = dot_rows(place_any, token_rows).astype(jnp.bfloat16)
        return swap_slots(filled)

    def swap_slots(slot_rows):
        swapped = lax.all_to_all(
            slot_rows.reshape(device_count, capacity, model_width),
            ("rows", "cols"),
            split_axis=0,
            concat_axis=0,
            tiled=True,
        )
        return swapped.reshape(device_count * capacity, model_width)

    cotangent_arrived = to_experts(cotangent)
    tokens_f = tokens_in.astype(jnp.float32)
    normed_low = layer_norm(tokens_f, ln1_gain, ln1_shift).astype(jnp.bfloat16)
    gathered = lax.all_gather(normed_low.reshape(-1, SEQ, model_width), "cols", axis=0, tiled=True)
    qkv_low, context_low, attn_parts = attention_forward(gathered, qkv_weight, out_weight)
    attn_ours, attn_theirs = share_over_cores(attn_parts, col_place)
    attn_out = attn_ours + attn_theirs
    hidden_one = tokens_f + attn_out
    mixed_low = layer_norm(hidden_one, ln2_gain, ln2_shift).astype(jnp.bfloat16)
    logits = jnp.dot(mixed_low, router_weight, preferred_element_type=jnp.float32)
    router_probs = jax.nn.softmax(logits, axis=-1)
    expert_ids = jnp.arange(experts, dtype=jnp.int32)
    chosen = (routes[:, :, None] == expert_ids[None, None, :]).astype(jnp.float32)
    gate_values = jnp.sum(router_probs[:, None, :] * chosen, axis=-1)
    grad_out = cotangent.astype(jnp.float32)
    mixed_sent, cotangent_arrived = lax.optimization_barrier((mixed_low, cotangent_arrived))
    arrived = to_experts(mixed_sent)
    own_expert = (row_place * lax.axis_size("cols") + col_place) // copies
    arrived_probs = jax.nn.softmax(
        jnp.dot(arrived, router_weight, preferred_element_type=jnp.float32), axis=-1
    )
    arrived_gate = jnp.sum(
        jnp.where(expert_ids[None, :] == own_expert, arrived_probs, 0.0), axis=-1, keepdims=True
    )
    grad_result = (arrived_gate * cotangent_arrived.astype(jnp.float32)).astype(jnp.bfloat16)
    pre_act = jnp.dot(arrived, expert_in, preferred_element_type=jnp.float32)
    act_low = jax.nn.gelu(pre_act, approximate=False).astype(jnp.bfloat16)
    result_low = jnp.dot(act_low, expert_out, preferred_element_type=jnp.float32).astype(
        jnp.bfloat16
    )
    returned = swap_slots(result_low)
    grad_act = dot_last(grad_result, expert_out)
    grad_pre_low = (grad_act * gelu_slope(pre_act)).astype(jnp.bfloat16)
    grad_arrived = dot_last(grad_pre_low, expert_in).astype(jnp.bfloat16)
    grad_sent = swap_slots(grad_arrived)
    arrived, grad_pre_low, act_low, grad_result, unused_rows = lax.optimization_barrier(
        (arrived, grad_pre_low, act_low, grad_result, grad_arrived)
    )
    first_grad = dot_rows(arrived, grad_pre_low)
    second_grad = dot_rows(act_low, grad_result)
    picked_one = jnp.dot(place_one, returned, preferred_element_type=jnp.float32)
    picked_two = jnp.dot(place_two, returned, preferred_element_type=jnp.float32)
    output = (
        hidden_one + gate_values[:, 0:1] * picked_one + gate_values[:, 1:2] * picked_two
    ).astype(jnp.bfloat16)
    grad_gates = jnp.stack(
        [jnp.sum(grad_out * picked_one, axis=-1), jnp.sum(grad_out * picked_two, axis=-1)], axis=1
    )
    grad_mixed_experts = jnp.dot(place_any, grad_sent, preferred_element_type=jnp.float32)
    gate_term = jnp.sum(grad_gates * gate_values, axis=-1, keepdims=True)
    grad_probs = jnp.sum(chosen * grad_gates[:, :, None], axis=1)
    grad_logits_low = (router_probs * (grad_probs - gate_term)).astype(jnp.bfloat16)
    router_grad = dot_rows(grad_logits_low, mixed_low)
    grad_mixed = dot_last(grad_logits_low, router_weight) + grad_mixed_experts
    unused_two, norm_two_back = jax.vjp(layer_norm, hidden_one, ln2_gain, ln2_shift)
    grad_hidden_part, ln2_gain_grad, ln2_shift_grad = norm_two_back(grad_mixed)
    grad_hidden = grad_out + grad_hidden_part
    grad_attn_low = grad_hidden.astype(jnp.bfloat16)
    grad_attn_all = lax.all_gather(
        grad_attn_low.reshape(-1, SEQ, model_width), "cols", axis=0, tiled=True
    )
    qkv_grad, out_grad, normed_parts = attention_backward(
        gathered, grad_attn_all, qkv_low, context_low, qkv_weight, out_weight
    )
    normed_ours, normed_theirs = share_over_cores(normed_parts, col_place)
    grad_normed = normed_ours.astype(jnp.float32) + normed_theirs.astype(jnp.float32)
    unused_one, norm_one_back = jax.vjp(layer_norm, tokens_f, ln1_gain, ln1_shift)
    grad_tokens_part, ln1_gain_grad, ln1_shift_grad = norm_one_back(grad_normed)
    tokens_grad = (grad_hidden + grad_tokens_part).astype(jnp.bfloat16)
    small_part = jnp.concatenate(
        [
            router_grad,
            ln1_gain_grad[None],
            ln1_shift_grad[None],
            ln2_gain_grad[None],
            ln2_shift_grad[None],
            jnp.zeros((4, model_width), jnp.float32),
        ],
        axis=0,
    )
    qkv_grad, out_grad, small_sum = sum_over_devices(
        qkv_grad, out_grad, small_part
    )
    router_grad = small_sum[:experts].T
    ln1_gain_grad, ln1_shift_grad, ln2_gain_grad, ln2_shift_grad = (
        small_sum[experts],
        small_sum[experts + 1],
        small_sum[experts + 2],
        small_sum[experts + 3],
    )
    return (
        output,
        tokens_grad,
        ln1_gain_grad,
        ln1_shift_grad,
        qkv_grad,
        out_grad,
        ln2_gain_grad,
        ln2_shift_grad,
        router_grad,
        first_grad,
        second_grad,
    )


def solution(mesh):
    in_specs = (
        P(("rows", "cols"), None),
        P(),
        P(),
        P(None, "cols"),
        P("cols", None),
        P(),
        P(),
        P(),
        P(None, ("rows", "cols")),
        P(("rows", "cols"), None),
        P(("rows", "cols"), None),
        P(("rows", "cols"), None),
    )
    out_specs = (
        P(("rows", "cols"), None),
        P(("rows", "cols"), None),
        P(),
        P(),
        P(None, "cols"),
        P("cols", None),
        P(),
        P(),
        P(),
        P(None, ("rows", "cols")),
        P(("rows", "cols"), None),
    )
    return jax.shard_map(body, mesh=mesh, in_specs=in_specs, out_specs=out_specs, check_vma=False)
```

```python
import jax
import jax.numpy as jnp
from jax import lax
from jax.experimental import pallas as pl
from jax.experimental.pallas import tpu as pltpu
from jax.sharding import PartitionSpec as P

DH = 64
FF = 3072
SEQ = 197


EPSILON = 1e-06


def layer_norm(values, norm_gain, norm_shift):
    average = jnp.mean(values, axis=-1, keepdims=True)
    centred = values - average
    variance = jnp.mean(centred * centred, axis=-1, keepdims=True)
    return centred * lax.rsqrt(variance + EPSILON) * norm_gain + norm_shift


def gelu_slope(pre_act):
    normal_cdf = 0.5 * (1.0 + jax.scipy.special.erf(pre_act * 0.7071067811865476))
    density = jnp.exp(-0.5 * pre_act * pre_act) * 0.3989422804014327
    return normal_cdf + pre_act * density


def dot_rows(first_side, second_side):
    return lax.dot_general(
        first_side, second_side, (((0,), (0,)), ((), ())), preferred_element_type=jnp.float32
    )


def dot_last(first_side, second_side):
    return lax.dot_general(
        first_side, second_side, (((1,), (1,)), ((), ())), preferred_element_type=jnp.float32
    )


def bit_orders(bits):
    cycle = list(range(bits - 1))
    return [cycle[turn:] + cycle[:turn] + [bits - 1] for turn in range(3)]


def sum_kernel(
    qkv_ref,
    out_ref,
    small_ref,
    qkv_sum,
    out_sum,
    small_sum,
    qkv_acc,
    out_acc,
    qkv_got,
    out_got,
    small_acc,
    small_got,
    send_sems,
    recv_sems,
    small_send,
    small_recv,
):
    shards = qkv_ref.shape[0]
    bits = shards.bit_length() - 1
    row_place = lax.axis_index("rows")
    col_place = lax.axis_index("cols")

    def row_partner(bit):
        here = (row_place // 2**bit) % 2
        return here, (row_place + (1 - 2 * here) * 2**bit, col_place)

    other_core = (row_place, 1 - col_place)
    barrier = pltpu.get_barrier_semaphore()
    for bit in range(bits):
        pl.semaphore_signal(
            barrier, inc=1, device_id=row_partner(bit)[1], device_id_type=pl.DeviceIdType.MESH
        )
    pl.semaphore_signal(
        barrier, inc=1, device_id=other_core, device_id_type=pl.DeviceIdType.MESH
    )
    pl.semaphore_wait(barrier, bits + 1)

    width = qkv_ref.shape[2]
    third = (width * qkv_ref.shape[1] + out_ref.shape[2] * out_ref.shape[1]) // (
        3 * qkv_ref.shape[1]
    )
    third = min(third // 128 * 128, width // 2)
    orders = bit_orders(bits)
    streams = [
        (qkv_ref, qkv_acc, qkv_got, qkv_sum, pl.ds(0, third), orders[0]),
        (qkv_ref, qkv_acc, qkv_got, qkv_sum, pl.ds(third, third), orders[1]),
        (out_ref, out_acc, out_got, out_sum, pl.ds(0, out_ref.shape[2]), orders[2]),
    ]
    if width > 2 * third:
        last = pl.ds(2 * third, width - 2 * third)
        streams.append((qkv_ref, qkv_acc, qkv_got, qkv_sum, last, orders[2]))
    bases = [0 for unused in streams]

    def send(source, target, place, step, device):
        copy = pltpu.make_async_remote_copy(
            src_ref=source,
            dst_ref=target,
            send_sem=send_sems.at[place, step],
            recv_sem=recv_sems.at[place, step],
            device_id=device,
            device_id_type=pl.DeviceIdType.MESH,
        )
        copy.start()
        return copy

    small_acc[0] = small_ref[...]

    def small_send_start(step):
        device = row_partner(step)[1] if step < bits else other_core
        copy = pltpu.make_async_remote_copy(
            src_ref=small_acc.at[step],
            dst_ref=small_got.at[step],
            send_sem=small_send.at[step],
            recv_sem=small_recv.at[step],
            device_id=device,
            device_id_type=pl.DeviceIdType.MESH,
        )
        copy.start()
        return copy

    def small_finish(step, copy):
        copy.wait()
        small_acc[step + 1] = small_acc[step] + small_got[step]

    def give_half(place, step):
        ref, acc, got, total, cols, order = streams[place]
        here, device = row_partner(order[step])
        half = shards >> (step + 1)
        source = ref if step == 0 else acc
        give = bases[place] + (1 - here) * half
        bases[place] = bases[place] + here * half
        return send(
            source.at[pl.ds(give, half), :, cols],
            got.at[pl.ds(shards - 2 * half, half), :, cols],
            place,
            step,
            device,
        )

    def pass_block(place, step):
        ref, acc, got, total, cols, order = streams[place]
        here, device = row_partner(order[step])
        held = shards >> (step + 1)
        block = total.at[pl.ds(bases[place], held), :, cols]
        bases[place] = bases[place] - here * held
        return send(block, block, place, 2 * bits - 1 - step, device)

    copies = [give_half(place, 0) for place in range(len(streams))]
    small_copy = small_send_start(0)
    for step in range(bits):
        half = shards >> (step + 1)
        for place, (ref, acc, got, total, cols, order) in enumerate(streams):
            copies[place].wait()
            source = ref if step == 0 else acc
            target = acc if step < bits - 1 else total
            keep = bases[place]

            def add(index, unused, parts=(source, target, got, cols, keep, shards - 2 * half)):
                source, target, got, cols, keep, start = parts
                target[keep + index, :, cols] = (
                    source[keep + index, :, cols].astype(jnp.float32)
                    + got[start + index, :, cols].astype(jnp.float32)
                ).astype(jnp.bfloat16)
                return unused

            lax.fori_loop(0, half, add, 0)
            if step < bits - 1:
                copies[place] = give_half(place, step + 1)
            else:
                copies[place] = pass_block(place, step)
        small_finish(step, small_copy)
        small_copy = small_send_start(step + 1)
    for step in reversed(range(bits)):
        for place in range(len(streams)):
            copies[place].wait()
            if step > 0:
                copies[place] = pass_block(place, step - 1)
    small_finish(bits, small_copy)
    small_sum[...] = small_acc[bits + 1]


def sum_over_devices(qkv_part, out_part, small_part):
    shards = lax.axis_size("rows")
    bits = shards.bit_length() - 1
    qkv_shape = (shards, qkv_part.shape[0] // shards, qkv_part.shape[1])
    out_shape = (shards, out_part.shape[0] // shards, out_part.shape[1])
    small_shape = small_part.shape
    in_vmem = pl.BlockSpec(memory_space=pltpu.VMEM)
    qkv_sum, out_sum, small_sum = pl.pallas_call(
        sum_kernel,
        out_shape=(
            jax.ShapeDtypeStruct(qkv_shape, jnp.bfloat16),
            jax.ShapeDtypeStruct(out_shape, jnp.bfloat16),
            jax.ShapeDtypeStruct(small_shape, jnp.float32),
        ),
        in_specs=[in_vmem] * 3,
        out_specs=(in_vmem,) * 3,
        scratch_shapes=[
            pltpu.VMEM(qkv_shape, jnp.bfloat16),
            pltpu.VMEM(out_shape, jnp.bfloat16),
            pltpu.VMEM(qkv_shape, jnp.bfloat16),
            pltpu.VMEM(out_shape, jnp.bfloat16),
            pltpu.VMEM((bits + 2, *small_shape), jnp.float32),
            pltpu.VMEM((bits + 1, *small_shape), jnp.float32),
            pltpu.SemaphoreType.DMA((4, 2 * bits)),
            pltpu.SemaphoreType.DMA((4, 2 * bits)),
            pltpu.SemaphoreType.DMA((bits + 1,)),
            pltpu.SemaphoreType.DMA((bits + 1,)),
        ],
        compiler_params=pltpu.CompilerParams(collective_id=0, has_side_effects=True),
        name="sum_gradients",
    )(qkv_part.reshape(qkv_shape), out_part.reshape(out_shape), small_part)
    return (
        qkv_sum.astype(jnp.float32).reshape(qkv_part.shape),
        out_sum.astype(jnp.float32).reshape(out_part.shape),
        small_sum,
    )


def dot_plain(first_side, second_side):
    return jnp.dot(first_side, second_side, preferred_element_type=jnp.float32)


def key_weights(queries, keys_all):
    scores = dot_last(keys_all, queries) * DH ** (-0.5)
    key_ids = lax.broadcasted_iota(jnp.int32, scores.shape, 0)
    scores = jnp.where(key_ids < SEQ, scores, -1e30)
    powers = jnp.exp(scores - jnp.max(scores, axis=0, keepdims=True))
    return powers * (1.0 / jnp.sum(powers, axis=0, keepdims=True))


def forward_kernel(rows_ref, qkv_weight, out_weight, qkv_ref, context_ref, parts_ref, padded):
    images = rows_ref.shape[0]
    span = padded.shape[0]
    heads = qkv_weight.shape[1] // (3 * DH)

    def one_image(image, unused):
        padded[...] = jnp.zeros_like(padded)
        padded[0:SEQ, :] = rows_ref[image]
        qkv_ref[image] = dot_plain(padded[...], qkv_weight[...]).astype(jnp.bfloat16)
        for pair in range(heads // 2):
            block = qkv_ref[image, :, 6 * DH * pair : 6 * DH * (pair + 1)]
            found = []
            for head in range(2):
                base = 3 * DH * head
                weights = key_weights(
                    block[:, base : base + DH], block[:, base + DH : base + 2 * DH]
                ).astype(jnp.bfloat16)
                found.append(dot_rows(weights, block[:, base + 2 * DH : base + 3 * DH]))
            context_ref[image, :, 2 * DH * pair : 2 * DH * (pair + 1)] = jnp.concatenate(
                found, axis=1
            ).astype(jnp.bfloat16)
        parts_ref[image] = dot_plain(context_ref[image], out_weight[...])[0:SEQ]
        return unused

    lax.fori_loop(0, images, one_image, 0)


def attention_forward(rows, qkv_weight, out_weight):
    images, unused, model_width = rows.shape
    span = -(-SEQ // 128) * 128
    in_vmem = pl.BlockSpec(memory_space=pltpu.VMEM)
    return pl.pallas_call(
        forward_kernel,
        out_shape=(
            jax.ShapeDtypeStruct((images, span, qkv_weight.shape[1]), jnp.bfloat16),
            jax.ShapeDtypeStruct((images, span, out_weight.shape[0]), jnp.bfloat16),
            jax.ShapeDtypeStruct((images, SEQ, model_width), jnp.float32),
        ),
        in_specs=[in_vmem] * 3,
        out_specs=(in_vmem,) * 3,
        scratch_shapes=[pltpu.VMEM((span, model_width), jnp.bfloat16)],
        name="attention_forward",
    )(rows, qkv_weight, out_weight)


def backward_kernel(
    rows_ref,
    grad_ref,
    qkv_ref,
    context_ref,
    qkv_weight,
    out_weight,
    qkv_grad,
    out_grad,
    normed_grad,
    rows_padded,
    grad_padded,
    grad_context,
    grad_qkv,
):
    images, span = qkv_ref.shape[0], qkv_ref.shape[1]
    heads = qkv_weight.shape[1] // (3 * DH)
    scale = DH ** (-0.5)
    rows_padded[...] = jnp.zeros_like(rows_padded)
    grad_padded[...] = jnp.zeros_like(grad_padded)

    def one_image(image, unused):
        rows_padded[image, 0:SEQ, :] = rows_ref[image]
        grad_padded[image, 0:SEQ, :] = grad_ref[image]
        grad_context[...] = dot_last(grad_padded[image], out_weight[...]).astype(jnp.bfloat16)
        for pair in range(heads // 2):
            block = qkv_ref[image, :, 6 * DH * pair : 6 * DH * (pair + 1)]
            grads = grad_context[:, 2 * DH * pair : 2 * DH * (pair + 1)]
            found = []
            for head in range(2):
                base = 3 * DH * head
                queries = block[:, base : base + DH]
                keys_all = block[:, base + DH : base + 2 * DH]
                values_all = block[:, base + 2 * DH : base + 3 * DH]
                head_grad = grads[:, DH * head : DH * (head + 1)]
                weights = key_weights(queries, keys_all)
                grad_values = dot_plain(weights.astype(jnp.bfloat16), head_grad)
                grad_weights = dot_last(values_all, head_grad)
                row_term = jnp.sum(grad_weights * weights, axis=0, keepdims=True)
                grad_scores = (weights * (grad_weights - row_term)).astype(jnp.bfloat16)
                grad_queries = dot_rows(grad_scores, keys_all) * scale
                grad_keys = dot_plain(grad_scores, queries) * scale
                found += [grad_queries, grad_keys, grad_values]
            grad_qkv[image, :, 6 * DH * pair : 6 * DH * (pair + 1)] = jnp.concatenate(
                found, axis=1
            ).astype(jnp.bfloat16)
        normed_grad[image] = dot_last(grad_qkv[image], qkv_weight[...])[0:SEQ].astype(jnp.bfloat16)
        return unused

    lax.fori_loop(0, images, one_image, 0)

    def flat(ref):
        return ref[...].reshape(images * span, ref.shape[2])

    qkv_grad[...] = dot_rows(flat(rows_padded), flat(grad_qkv)).astype(jnp.bfloat16)
    out_grad[...] = dot_rows(flat(context_ref), flat(grad_padded)).astype(jnp.bfloat16)


def attention_backward(rows, grad_rows, qkv, context, qkv_weight, out_weight):
    images, unused, model_width = rows.shape
    span = qkv.shape[1]
    in_vmem = pl.BlockSpec(memory_space=pltpu.VMEM)
    return pl.pallas_call(
        backward_kernel,
        out_shape=(
            jax.ShapeDtypeStruct(qkv_weight.shape, jnp.bfloat16),
            jax.ShapeDtypeStruct(out_weight.shape, jnp.bfloat16),
            jax.ShapeDtypeStruct((images, SEQ, model_width), jnp.bfloat16),
        ),
        in_specs=[in_vmem] * 6,
        out_specs=(in_vmem,) * 3,
        scratch_shapes=[
            pltpu.VMEM((images, span, model_width), jnp.bfloat16),
            pltpu.VMEM((images, span, model_width), jnp.bfloat16),
            pltpu.VMEM((span, out_weight.shape[0]), jnp.bfloat16),
            pltpu.VMEM((images, span, qkv_weight.shape[1]), jnp.bfloat16),
        ],
        name="attention_backward",
    )(rows, grad_rows, qkv, context, qkv_weight, out_weight)


def share_over_cores(parts, col_place):
    count = parts.shape[0] // 2
    theirs = lax.dynamic_slice_in_dim(parts, (1 - col_place) * count, count, 0)
    ours = lax.dynamic_slice_in_dim(parts, col_place * count, count, 0)
    theirs = theirs.reshape(count * SEQ, -1)
    ours = ours.reshape(count * SEQ, -1)
    return ours, lax.ppermute(theirs, "cols", [(0, 1), (1, 0)])


def body(
    tokens_in,
    ln1_gain,
    ln1_shift,
    qkv_weight,
    out_weight,
    ln2_gain,
    ln2_shift,
    router_weight,
    expert_in,
    expert_out,
    routes,
    cotangent,
):
    local_rows = tokens_in.shape[0]
    model_width = tokens_in.shape[1]
    experts = router_weight.shape[1]
    capacity = max(2, 8 * local_rows // (3 * experts))
    row_place = lax.axis_index("rows")
    col_place = lax.axis_index("cols")
    device_count = lax.axis_size("rows") * lax.axis_size("cols")
    copies = device_count // experts
    slot_ids = jnp.arange(device_count * capacity, dtype=jnp.int32)
    slot_expert = slot_ids // (capacity * copies)
    names_slot = [routes[:, k][:, None] == slot_expert[None, :] for k in range(2)]
    token_ids = jnp.arange(local_rows, dtype=jnp.int32)
    earlier = (token_ids[None, :] < token_ids[:, None]).astype(jnp.bfloat16)
    slot_ranks = jnp.dot(
        earlier,
        (names_slot[0] | names_slot[1]).astype(jnp.bfloat16),
        preferred_element_type=jnp.float32,
    )
    in_slot = slot_ranks == (slot_ids % capacity).astype(jnp.float32)[None, :]
    place_one = (names_slot[0] & in_slot).astype(jnp.bfloat16)
    place_two = (names_slot[1] & in_slot).astype(jnp.bfloat16)
    place_any = place_one + place_two

    def to_experts(token_rows):
        filled = dot_rows(place_any, token_rows).astype(jnp.bfloat16)
        return swap_slots(filled)

    def swap_slots(slot_rows):
        swapped = lax.all_to_all(
            slot_rows.reshape(device_count, capacity, slot_rows.shape[1]),
            ("rows", "cols"),
            split_axis=0,
            concat_axis=0,
            tiled=True,
        )
        return swapped.reshape(slot_rows.shape)

    tokens_f = tokens_in.astype(jnp.float32)
    normed_low = layer_norm(tokens_f, ln1_gain, ln1_shift).astype(jnp.bfloat16)
    gathered = lax.all_gather(normed_low.reshape(-1, SEQ, model_width), "cols", axis=0, tiled=True)
    qkv_low, context_low, attn_parts = attention_forward(gathered, qkv_weight, out_weight)
    attn_ours, attn_theirs = share_over_cores(attn_parts, col_place)
    attn_out = attn_ours + attn_theirs
    hidden_one = tokens_f + attn_out
    mixed_low = layer_norm(hidden_one, ln2_gain, ln2_shift).astype(jnp.bfloat16)
    logits = jnp.dot(mixed_low, router_weight, preferred_element_type=jnp.float32)
    router_probs = jax.nn.softmax(logits, axis=-1)
    expert_ids = jnp.arange(experts, dtype=jnp.int32)
    chosen = (routes[:, :, None] == expert_ids[None, None, :]).astype(jnp.float32)
    gate_values = jnp.sum(router_probs[:, None, :] * chosen, axis=-1)
    grad_out = cotangent.astype(jnp.float32)
    arrived = to_experts(mixed_low)
    cotangent_sent, unused_rows = lax.optimization_barrier((cotangent, mixed_low))
    cotangent_arrived = to_experts(cotangent_sent)
    own_expert = (row_place * lax.axis_size("cols") + col_place) // copies
    arrived_probs = jax.nn.softmax(
        jnp.dot(arrived, router_weight, preferred_element_type=jnp.float32), axis=-1
    )
    arrived_gate = jnp.sum(
        jnp.where(expert_ids[None, :] == own_expert, arrived_probs, 0.0), axis=-1, keepdims=True
    )
    grad_result = (arrived_gate * cotangent_arrived.astype(jnp.float32)).astype(jnp.bfloat16)
    pre_act = jnp.dot(arrived, expert_in, preferred_element_type=jnp.float32)
    act_low = jax.nn.gelu(pre_act, approximate=False).astype(jnp.bfloat16)
    result_low = jnp.dot(act_low, expert_out, preferred_element_type=jnp.float32).astype(
        jnp.bfloat16
    )
    gate_slots = jnp.sum(
        cotangent_arrived.astype(jnp.float32) * result_low.astype(jnp.float32),
        axis=-1,
        keepdims=True,
    )
    gate_high = lax.reduce_precision(gate_slots, 8, 7)
    gate_middle = lax.reduce_precision(gate_slots - gate_high, 8, 7)
    gate_low = gate_slots - gate_high - gate_middle
    lanes = jnp.arange(128, dtype=jnp.int32)[None, :]
    gate_lanes = jnp.where(
        lanes == 0,
        gate_high,
        jnp.where(lanes == 1, gate_middle, jnp.where(lanes == 2, gate_low, 0.0)),
    ).astype(jnp.bfloat16)
    grad_act = dot_last(grad_result, expert_out)
    grad_pre_low = (grad_act * gelu_slope(pre_act)).astype(jnp.bfloat16)
    grad_arrived = dot_last(grad_pre_low, expert_in).astype(jnp.bfloat16)
    grad_sent = swap_slots(jnp.concatenate([grad_arrived, gate_lanes], axis=1))
    arrived, grad_pre_low, act_low, grad_result, unused_rows = lax.optimization_barrier(
        (arrived, grad_pre_low, act_low, grad_result, grad_arrived)
    )
    first_grad = dot_rows(arrived, grad_pre_low)
    second_grad = dot_rows(act_low, grad_result)
    gates_sent = grad_sent[:, model_width:]
    grad_gates = jnp.stack(
        [
            jnp.sum(jnp.dot(place, gates_sent, preferred_element_type=jnp.float32), axis=-1)
            for place in (place_one, place_two)
        ],
        axis=1,
    )
    grad_mixed_experts = jnp.dot(
        place_any, grad_sent[:, :model_width], preferred_element_type=jnp.float32
    )
    result_sent, unused_sent = lax.optimization_barrier((result_low, grad_sent))
    returned = swap_slots(result_sent)
    picked_one = jnp.dot(place_one, returned, preferred_element_type=jnp.float32)
    picked_two = jnp.dot(place_two, returned, preferred_element_type=jnp.float32)
    output = (
        hidden_one + gate_values[:, 0:1] * picked_one + gate_values[:, 1:2] * picked_two
    ).astype(jnp.bfloat16)
    gate_term = jnp.sum(grad_gates * gate_values, axis=-1, keepdims=True)
    grad_probs = jnp.sum(chosen * grad_gates[:, :, None], axis=1)
    grad_logits_low = (router_probs * (grad_probs - gate_term)).astype(jnp.bfloat16)
    router_grad = dot_rows(grad_logits_low, mixed_low)
    grad_mixed = dot_last(grad_logits_low, router_weight) + grad_mixed_experts
    unused_two, norm_two_back = jax.vjp(layer_norm, hidden_one, ln2_gain, ln2_shift)
    grad_hidden_part, ln2_gain_grad, ln2_shift_grad = norm_two_back(grad_mixed)
    grad_hidden = grad_out + grad_hidden_part
    grad_attn_low = grad_hidden.astype(jnp.bfloat16)
    grad_attn_all = lax.all_gather(
        grad_attn_low.reshape(-1, SEQ, model_width), "cols", axis=0, tiled=True
    )
    qkv_grad, out_grad, normed_parts = attention_backward(
        gathered, grad_attn_all, qkv_low, context_low, qkv_weight, out_weight
    )
    normed_ours, normed_theirs = share_over_cores(normed_parts, col_place)
    grad_normed = normed_ours.astype(jnp.float32) + normed_theirs.astype(jnp.float32)
    unused_one, norm_one_back = jax.vjp(layer_norm, tokens_f, ln1_gain, ln1_shift)
    grad_tokens_part, ln1_gain_grad, ln1_shift_grad = norm_one_back(grad_normed)
    tokens_grad = (grad_hidden + grad_tokens_part).astype(jnp.bfloat16)
    small_part = jnp.concatenate(
        [
            router_grad,
            ln1_gain_grad[None],
            ln1_shift_grad[None],
            ln2_gain_grad[None],
            ln2_shift_grad[None],
            jnp.zeros((4, model_width), jnp.float32),
        ],
        axis=0,
    )
    qkv_grad, out_grad, small_sum = sum_over_devices(
        qkv_grad, out_grad, small_part
    )
    router_grad = small_sum[:experts].T
    ln1_gain_grad, ln1_shift_grad, ln2_gain_grad, ln2_shift_grad = (
        small_sum[experts],
        small_sum[experts + 1],
        small_sum[experts + 2],
        small_sum[experts + 3],
    )
    return (
        output,
        tokens_grad,
        ln1_gain_grad,
        ln1_shift_grad,
        qkv_grad,
        out_grad,
        ln2_gain_grad,
        ln2_shift_grad,
        router_grad,
        first_grad,
        second_grad,
    )


def solution(mesh):
    in_specs = (
        P(("rows", "cols"), None),
        P(),
        P(),
        P(None, "cols"),
        P("cols", None),
        P(),
        P(),
        P(),
        P(None, ("rows", "cols")),
        P(("rows", "cols"), None),
        P(("rows", "cols"), None),
        P(("rows", "cols"), None),
    )
    out_specs = (
        P(("rows", "cols"), None),
        P(("rows", "cols"), None),
        P(),
        P(),
        P(None, "cols"),
        P("cols", None),
        P(),
        P(),
        P(),
        P(None, ("rows", "cols")),
        P(("rows", "cols"), None),
    )
    return jax.shard_map(body, mesh=mesh, in_specs=in_specs, out_specs=out_specs, check_vma=False)
```
